32 devices in a mesh: parts: 2 (over y), dp: 4 (over z), tensor: 2 (over x), group: 2 (over core).
Axes of the slice: x: 2, y: 2, z: 4, core: 2. Of those that a mesh axis runs over, the one named last changes fastest.
Arguments:
- activations: bfloat16 [1, 32, 256, 4096], P(None, ('parts', 'dp'), None, ('tensor', 'group')), parts along dimension 1, may hold values from -6 to 6
- out_grads: bfloat16 [1, 32, 256, 14336], P(None, ('parts', 'dp'), None, ('tensor', 'group')), parts along dimension 1, may hold values from -6 to 6
- proj_in: bfloat16 [1, 4096, 64], P(None, ('tensor', 'group')), may hold values from -0.09375 to 0.09375
- proj_out: bfloat16 [1, 14336, 64], P(None, ('tensor', 'group')), may hold values from -0.046875 to 0.046875
- queries: bfloat16 [4096, 4096], P(('parts', 'tensor', 'group'), 'dp'), parts along dimension 0, may hold values from -0.005859375 to 0.005859375
Outputs:
- scores: float32 [16, 4096], P('dp', ('parts', 'tensor', 'group')), parts along dimension 1
The draws below stay inside these ranges and needn't reach their ends.
There are 2 independent parts, one for each index of `parts`. The reference program is written for one: setup_inputs(seed, part) draws one part's arguments, and reference() takes and returns one part's arrays. A program takes and returns all parts, laid end to end along the dimension named above; an argument that names none is the same for every part. Nothing has to cross between parts.
All inputs are finite; a program needn't handle non-finite values.
Results may differ from the reference program's by a relative error of at most 0.005.
Values may be sent and summed in bfloat16 or wider, within the bound.
A program may use at most 64 MiB of HBM per device.

```python
import jax
import jax.numpy as jnp
from jax import lax

D = 4096
FF = 14336
RANK = 64
LAYERS = 1
TOK = 256
SEQS = 16
QUERIES = 2048
FEAT = 4096


def shard_levels(stream_key, shape, shards, low, top_value):
    gain, own = 1.0, jax.random.fold_in(stream_key, 6)
    for axis_at, parts in shards:
        draws = jnp.exp(jax.random.uniform(jax.random.fold_in(own, axis_at), (parts,), jnp.float32, low / len(shards), top_value / len(shards)))
        gain = gain * jnp.repeat(draws, shape[axis_at] // parts).reshape([-1 if axis == axis_at else 1 for axis in range(len(shape))])
    return gain


def gaussian(stream_key, dims, spread, most, shards=(), held_as=jnp.bfloat16):
    drawn = spread * jax.random.normal(stream_key, dims, jnp.float32)
    if shards:
        drawn = drawn * shard_levels(stream_key, dims, shards, -0.22, 0.18)
    return jnp.clip(drawn, -most, most).astype(held_as)


def setup_inputs(seed: int = 0, part: int = 0) -> dict:
    splits = jax.random.split(jax.random.key(seed), 6)
    part_splits = jax.random.split(jax.random.fold_in(splits[5], part), 6)
    return {
        "activations": gaussian(part_splits[0], (LAYERS, SEQS, TOK, D), 1.0, 6.0, ((1, 4), (3, 4))),
        "out_grads": gaussian(part_splits[1], (LAYERS, SEQS, TOK, FF), 1.0, 6.0, ((1, 4), (3, 4))),
        "proj_in": gaussian(splits[2], (LAYERS, D, RANK), D ** -0.5, 0.09375, ((1, 4),)),
        "proj_out": gaussian(splits[3], (LAYERS, FF, RANK), FF ** -0.5, 0.046875, ((1, 4),)),
        "queries": gaussian(part_splits[4], (QUERIES, FEAT), (TOK * FEAT) ** -0.5, 0.005859375, ((0, 4), (1, 4))),
    }


def layer_grads(items):
    acts_layer, grads_layer, in_layer, out_layer = items
    proj_acts = jnp.einsum("sth,hr->str", acts_layer.astype(jnp.float32), in_layer.astype(jnp.float32)).astype(jnp.bfloat16)
    proj_grads = jnp.einsum("sth,hr->str", grads_layer.astype(jnp.float32), out_layer.astype(jnp.float32)).astype(jnp.bfloat16)
    return jnp.einsum("sta,stb->sab", proj_grads.astype(jnp.float32), proj_acts.astype(jnp.float32)).astype(jnp.bfloat16)


def reference(activations, out_grads, proj_in, proj_out, queries):
    stacked = lax.map(layer_grads, (activations, out_grads, proj_in, proj_out))
    example_grads = jnp.transpose(stacked, (1, 0, 2, 3)).reshape(stacked.shape[1], -1)
    return lax.dot_general(example_grads, queries, (((1,), (1,)), ((), ())), preferred_element_type=jnp.float32)
```

```python
import functools
import itertools

import jax
import jax.numpy as jnp
from jax import lax
from jax.experimental import pallas as pl
from jax.experimental.pallas import tpu as pltpu
from jax.sharding import PartitionSpec as P

MESH = pl.DeviceIdType.MESH
WIRE = jnp.bfloat16
NT = (((1,), (1,)), ((), ()))
LANES = 128


def shards(activations, out_grads, proj_in, proj_out, queries):
    proj_acts = jnp.einsum(
        "lsth,lhr->lstr", activations, proj_in, preferred_element_type=jnp.float32
    )
    proj_grads = jnp.einsum(
        "lsth,lhr->lstr", out_grads, proj_out, preferred_element_type=jnp.float32
    )
    summed_acts, summed_grads = lax.psum((proj_acts, proj_grads), ("tensor", "group"))
    outer = jnp.einsum(
        "lsta,lstb->slab",
        summed_grads.astype(jnp.bfloat16),
        summed_acts.astype(jnp.bfloat16),
        preferred_element_type=jnp.float32,
    )
    seq_count = outer.shape[0]
    example_grads = outer.reshape(seq_count, -1).astype(jnp.bfloat16)
    traded = lax.all_to_all(example_grads, "dp", split_axis=1, concat_axis=0, tiled=True)
    return lax.psum_scatter(
        lax.dot_general(
            traded, queries, (((1,), (1,)), ((), ())), preferred_element_type=jnp.float32
        ),
        "dp",
        scatter_dimension=0,
        tiled=True,
    )


def dot(left, right):
    return lax.dot_general(left, right, NT, preferred_element_type=jnp.float32)


def kernel(
    sizes,
    acts_hbm, grads_hbm, in_hbm, out_hbm, queries_hbm, scores_ref,
    acts, grads, w_in, w_out, queries, paired, own, sent, got, mine, feats, part, back,
    load_sem, send1, recv1, send2, recv2, send3, recv3,
):
    nd, nt, ng = sizes
    seqs, rank = nt * ng, w_in.shape[0]
    half = rank // 2
    d, t, g = lax.axis_index("dp"), lax.axis_index("tensor"), lax.axis_index("group")

    def peer(rd, rt, rg):
        return lax.rem(d + rd, nd), lax.rem(t + rt, nt), lax.rem(g + rg, ng)

    def device(where):
        return {"dp": where[0], "tensor": where[1], "group": where[2]}

    turns = sorted(itertools.product(range(nt), range(ng)), reverse=True)
    others = [r for r in itertools.product(range(nd), range(nt), range(ng)) if any(r)]
    others.sort(key=lambda r: (-min(r[0], nd - r[0]), -r[1], -r[2]))

    loads = [
        pltpu.make_async_copy(in_hbm, w_in, load_sem.at[0]),
        pltpu.make_async_copy(out_hbm, w_out, load_sem.at[1]),
    ]
    seq_loads = []
    for slot, (rt, rg) in enumerate(turns):
        _, pt, pg = peer(0, rt, rg)
        seq = pt * ng + pg
        seq_loads.append((
            pltpu.make_async_copy(acts_hbm.at[0, seq], acts.at[slot], load_sem.at[3 + 2 * slot]),
            pltpu.make_async_copy(grads_hbm.at[0, seq], grads.at[slot], load_sem.at[4 + 2 * slot]),
        ))
    query_load = pltpu.make_async_copy(queries_hbm, queries, load_sem.at[2])
    for copy in loads:
        copy.start()
    for pair in seq_loads:
        for copy in pair:
            copy.start()
    query_load.start()

    barrier = pltpu.get_barrier_semaphore()
    for r in others:
        pl.semaphore_signal(barrier, inc=1, device_id=device(peer(*r)), device_id_type=MESH)

    row = lax.broadcasted_iota(jnp.int32, (rank, rank), 0)
    column = lax.broadcasted_iota(jnp.int32, (rank, rank), 1)
    source = jnp.where(row < half, 2 * row, 2 * (row - half) + 1)
    pick = (column == source).astype(jnp.bfloat16)
    loads[1].wait()
    paired[...] = jnp.dot(
        pick, w_out[...], preferred_element_type=jnp.float32
    ).astype(jnp.bfloat16)
    loads[0].wait()

    first = []
    for slot, (rt, rg) in enumerate(turns):
        seq_loads[slot][0].wait()
        part_acts = dot(w_in[...], acts[slot])
        seq_loads[slot][1].wait()
        part_grads = dot(paired[...], grads[slot])
        if (rt, rg) == (0, 0):
            own[:rank] = part_acts
            own[rank:] = part_grads
            continue
        sent[slot, :rank] = part_acts.astype(sent.dtype)
        sent[slot, rank:] = part_grads.astype(sent.dtype)
        if not first:
            pl.semaphore_wait(barrier, len(others))
        copy = pltpu.make_async_remote_copy(
            src_ref=sent.at[slot],
            dst_ref=got.at[slot],
            send_sem=send1.at[slot],
            recv_sem=recv1.at[slot],
            device_id=device(peer(0, rt, rg)),
            device_id_type=MESH,
        )
        copy.start()
        first.append(copy)

    total = own[...]
    for slot, copy in enumerate(first):
        copy.wait_recv()
        total = total + got[slot].astype(jnp.float32)
    summed = total.astype(jnp.bfloat16)
    twice = jnp.concatenate([summed[:rank], summed[:rank]], axis=0)
    outer = dot(summed[rank:], twice)
    lane = lax.broadcasted_iota(jnp.int32, (half, 2 * rank), 1)
    eg = jnp.where(lane < rank, outer[:half], outer[half:])
    eg = eg.astype(jnp.bfloat16).astype(jnp.float32)
    deep = half // nd
    for other in range(nd):
        mine[other] = eg[other * deep:(other + 1) * deep]

    me = (d * nt + t) * ng + g
    second = []
    for at, r in enumerate(others):
        where = peer(*r)
        copy = pltpu.make_async_remote_copy(
            src_ref=mine.at[where[0]],
            dst_ref=feats.at[me],
            send_sem=send2.at[at],
            recv_sem=recv2.at[at],
            device_id=device(where),
            device_id_type=MESH,
        )
        copy.start()
        second.append(copy)
    feats[me] = mine[d]
    query_load.wait()
    for copy in second:
        copy.wait_recv()
    flat = jnp.concatenate([feats[:, k, :] for k in range(deep)], axis=1).astype(jnp.bfloat16)
    scores = dot(flat, queries[...])
    for other in range(nd):
        part[other] = scores[other * seqs:(other + 1) * seqs]

    third = []
    for rd in sorted(range(1, nd), key=lambda r: -min(r, nd - r)):
        where = peer(rd, 0, 0)
        copy = pltpu.make_async_remote_copy(
            src_ref=part.at[where[0]],
            dst_ref=back.at[rd - 1],
            send_sem=send3.at[rd - 1],
            recv_sem=recv3.at[rd - 1],
            device_id=device(where),
            device_id_type=MESH,
        )
        copy.start()
        third.append((rd, copy))
    result = part[d]
    for rd, copy in reversed(third):
        copy.wait_recv()
        result = result + back[rd - 1]
    scores_ref[...] = result
    for copy in first + second + [copy for _, copy in third]:
        copy.wait_send()


def fused(sizes, activations, out_grads, proj_in, proj_out, queries):
    nd, nt, ng = sizes
    seqs, tokens, width = activations.shape[1:]
    hidden, rank = out_grads.shape[3], proj_in.shape[2]
    asked, local = queries.shape
    everyone = nd * seqs
    deep = rank // 2 // nd
    bf16, f32 = jnp.bfloat16, jnp.float32
    dma = pltpu.SemaphoreType.DMA
    hbm = pl.BlockSpec(memory_space=pl.ANY)
    return pl.pallas_call(
        functools.partial(kernel, sizes),
        out_shape=jax.ShapeDtypeStruct((seqs, asked), f32),
        in_specs=[hbm] * 5,
        out_specs=pl.BlockSpec(memory_space=pltpu.VMEM),
        scratch_shapes=[
            pltpu.VMEM((seqs, tokens, width), bf16),
            pltpu.VMEM((seqs, tokens, hidden), bf16),
            pltpu.VMEM((rank, width), bf16),
            pltpu.VMEM((rank, hidden), bf16),
            pltpu.VMEM((asked, local), bf16),
            pltpu.VMEM((rank, hidden), bf16),
            pltpu.VMEM((2 * rank, tokens), f32),
            pltpu.VMEM((seqs, 2 * rank, tokens), WIRE),
            pltpu.VMEM((seqs, 2 * rank, tokens), WIRE),
            pltpu.VMEM((nd, deep, LANES), f32),
            pltpu.VMEM((everyone, deep, LANES), f32),
            pltpu.VMEM((nd, seqs, asked), f32),
            pltpu.VMEM((nd, seqs, asked), f32),
            dma((3 + 2 * seqs,)),
            dma((seqs,)), dma((seqs,)),
            dma((everyone,)), dma((everyone,)),
            dma((nd,)), dma((nd,)),
        ],
        compiler_params=pltpu.CompilerParams(
            collective_id=0, has_side_effects=True, vmem_limit_bytes=60 * 2**20
        ),
        name="scores",
    )(
        activations,
        out_grads,
        jnp.swapaxes(proj_in[0], 0, 1),
        jnp.swapaxes(proj_out[0], 0, 1),
        queries,
    )


def solution(mesh):
    placed = (
        P(None, ("parts", "dp"), None, ("tensor", "group")),
        P(None, ("parts", "dp"), None, ("tensor", "group")),
        P(None, ("tensor", "group"), None),
        P(None, ("tensor", "group"), None),
        P(("parts", "tensor", "group"), "dp"),
    )
    sizes = mesh.shape["dp"], mesh.shape["tensor"], mesh.shape["group"]

    def body(activations, out_grads, proj_in, proj_out, queries):
        layers, seqs = activations.shape[:2]
        rank = proj_in.shape[2]
        fits = (
            layers == 1
            and seqs == sizes[1] * sizes[2]
            and 2 * rank == LANES
            and rank % (2 * sizes[0]) == 0
        )
        run = functools.partial(fused, sizes) if fits else shards
        return run(activations, out_grads, proj_in, proj_out, queries)

    return jax.shard_map(
        body,
        mesh=mesh,
        in_specs=placed,
        out_specs=P("dp", ("parts", "tensor", "group")),
        check_vma=False,
    )
```

```python
import functools
import itertools

import jax
import jax.numpy as jnp
from jax import lax
from jax.experimental import pallas as pl
from jax.experimental.pallas import tpu as pltpu
from jax.sharding import PartitionSpec as P

MESH = pl.DeviceIdType.MESH
WIRE = jnp.bfloat16
NT = (((1,), (1,)), ((), ()))
LANES = 128


def shards(activations, out_grads, proj_in, proj_out, queries):
    proj_acts = jnp.einsum(
        "lsth,lhr->lstr", activations, proj_in, preferred_element_type=jnp.float32
    )
    proj_grads = jnp.einsum(
        "lsth,lhr->lstr", out_grads, proj_out, preferred_element_type=jnp.float32
    )
    summed_acts, summed_grads = lax.psum((proj_acts, proj_grads), ("tensor", "group"))
    outer = jnp.einsum(
        "lsta,lstb->slab",
        summed_grads.astype(jnp.bfloat16),
        summed_acts.astype(jnp.bfloat16),
        preferred_element_type=jnp.float32,
    )
    seq_count = outer.shape[0]
    example_grads = outer.reshape(seq_count, -1).astype(jnp.bfloat16)
    traded = lax.all_to_all(example_grads, "dp", split_axis=1, concat_axis=0, tiled=True)
    return lax.psum_scatter(
        lax.dot_general(
            traded, queries, (((1,), (1,)), ((), ())), preferred_element_type=jnp.float32
        ),
        "dp",
        scatter_dimension=0,
        tiled=True,
    )


def dot(left, right):
    return lax.dot_general(left, right, NT, preferred_element_type=jnp.float32)


def kernel(
    sizes,
    acts_hbm, grads_hbm, in_hbm, out_hbm, queries_hbm, scores_ref,
    acts, grads, w_in, w_out, queries, paired, own, sent, got, mine, feats, part, back,
    load_sem, send1, recv1, send2, recv2, send3, recv3,
):
    nd, nt, ng = sizes
    seqs, rank = nt * ng, w_in.shape[0]
    half = rank // 2
    d, t, g = lax.axis_index("dp"), lax.axis_index("tensor"), lax.axis_index("group")

    def peer(rd, rt, rg):
        return lax.rem(d + rd, nd), lax.rem(t + rt, nt), lax.rem(g + rg, ng)

    def device(where):
        return {"dp": where[0], "tensor": where[1], "group": where[2]}

    turns = sorted(itertools.product(range(nt), range(ng)), reverse=True)
    others = [r for r in itertools.product(range(nd), range(nt), range(ng)) if any(r)]
    others.sort(key=lambda r: (-min(r[0], nd - r[0]), -r[1], -r[2]))

    loads = [
        pltpu.make_async_copy(in_hbm, w_in, load_sem.at[0]),
        pltpu.make_async_copy(out_hbm, w_out, load_sem.at[1]),
    ]
    seq_loads = []
    for slot, (rt, rg) in enumerate(turns):
        _, pt, pg = peer(0, rt, rg)
        seq = pt * ng + pg
        seq_loads.append((
            pltpu.make_async_copy(acts_hbm.at[0, seq], acts.at[slot], load_sem.at[3 + 2 * slot]),
            pltpu.make_async_copy(grads_hbm.at[0, seq], grads.at[slot], load_sem.at[4 + 2 * slot]),
        ))
    query_load = pltpu.make_async_copy(queries_hbm, queries, load_sem.at[2])
    barrier = pltpu.get_barrier_semaphore()
    for r in others:
        pl.semaphore_signal(barrier, inc=1, device_id=device(peer(*r)), device_id_type=MESH)

    for copy in loads:
        copy.start()
    for pair in seq_loads:
        for copy in pair:
            copy.start()
    query_load.start()

    row = lax.broadcasted_iota(jnp.int32, (rank, rank), 0)
    column = lax.broadcasted_iota(jnp.int32, (rank, rank), 1)
    source = jnp.where(row < half, 2 * row, 2 * (row - half) + 1)
    pick = (column == source).astype(jnp.bfloat16)
    loads[1].wait()
    paired[...] = jnp.dot(
        pick, w_out[...], preferred_element_type=jnp.float32
    ).astype(jnp.bfloat16)
    loads[0].wait()

    first = []
    for slot, (rt, rg) in enumerate(turns):
        seq_loads[slot][0].wait()
        seq_loads[slot][1].wait()
        part_acts = dot(w_in[...], acts[slot])
        part_grads = dot(paired[...], grads[slot])
        if (rt, rg) == (0, 0):
            own[:rank] = part_acts
            own[rank:] = part_grads
            continue
        sent[slot, :rank] = part_acts.astype(sent.dtype)
        sent[slot, rank:] = part_grads.astype(sent.dtype)
        if not first:
            pl.semaphore_wait(barrier, len(others))
        copy = pltpu.make_async_remote_copy(
            src_ref=sent.at[slot],
            dst_ref=got.at[slot],
            send_sem=send1.at[slot],
            recv_sem=recv1.at[slot],
            device_id=device(peer(0, rt, rg)),
            device_id_type=MESH,
        )
        copy.start()
        first.append(copy)

    total = own[...]
    for slot, copy in enumerate(first):
        copy.wait_recv()
        total = total + got[slot].astype(jnp.float32)
    summed = total.astype(jnp.bfloat16)
    twice = jnp.concatenate([summed[:rank], summed[:rank]], axis=0)
    outer = dot(summed[rank:], twice)
    lane = lax.broadcasted_iota(jnp.int32, (half, 2 * rank), 1)
    eg = jnp.where(lane < rank, outer[:half], outer[half:])
    eg = eg.astype(jnp.bfloat16).astype(jnp.float32)
    deep = half // nd
    for other in range(nd):
        mine[other] = eg[other * deep:(other + 1) * deep]

    me = (d * nt + t) * ng + g
    second = []
    for at, r in enumerate(others):
        where = peer(*r)
        copy = pltpu.make_async_remote_copy(
            src_ref=mine.at[where[0]],
            dst_ref=feats.at[me],
            send_sem=send2.at[at],
            recv_sem=recv2.at[at],
            device_id=device(where),
            device_id_type=MESH,
        )
        copy.start()
        second.append(copy)
    feats[me] = mine[d]
    query_load.wait()
    for copy in second:
        copy.wait_recv()
    flat = jnp.concatenate([feats[:, k, :] for k in range(deep)], axis=1).astype(jnp.bfloat16)
    scores = dot(flat, queries[...])
    for other in range(nd):
        part[other] = scores[other * seqs:(other + 1) * seqs]

    third = []
    for rd in sorted(range(1, nd), key=lambda r: -min(r, nd - r)):
        where = peer(rd, 0, 0)
        copy = pltpu.make_async_remote_copy(
            src_ref=part.at[where[0]],
            dst_ref=back.at[rd - 1],
            send_sem=send3.at[rd - 1],
            recv_sem=recv3.at[rd - 1],
            device_id=device(where),
            device_id_type=MESH,
        )
        copy.start()
        third.append((rd, copy))
    result = part[d]
    for rd, copy in reversed(third):
        copy.wait_recv()
        result = result + back[rd - 1]
    scores_ref[...] = result
    for copy in first + second + [copy for _, copy in third]:
        copy.wait_send()


def fused(sizes, activations, out_grads, proj_in, proj_out, queries):
    nd, nt, ng = sizes
    seqs, tokens, width = activations.shape[1:]
    hidden, rank = out_grads.shape[3], proj_in.shape[2]
    asked, local = queries.shape
    everyone = nd * seqs
    deep = rank // 2 // nd
    bf16, f32 = jnp.bfloat16, jnp.float32
    dma = pltpu.SemaphoreType.DMA
    hbm = pl.BlockSpec(memory_space=pl.ANY)
    return pl.pallas_call(
        functools.partial(kernel, sizes),
        out_shape=jax.ShapeDtypeStruct((seqs, asked), f32),
        in_specs=[hbm] * 5,
        out_specs=pl.BlockSpec(memory_space=pltpu.VMEM),
        scratch_shapes=[
            pltpu.VMEM((seqs, tokens, width), bf16),
            pltpu.VMEM((seqs, tokens, hidden), bf16),
            pltpu.VMEM((rank, width), bf16),
            pltpu.VMEM((rank, hidden), bf16),
            pltpu.VMEM((asked, local), bf16),
            pltpu.VMEM((rank, hidden), bf16),
            pltpu.VMEM((2 * rank, tokens), f32),
            pltpu.VMEM((seqs, 2 * rank, tokens), WIRE),
            pltpu.VMEM((seqs, 2 * rank, tokens), WIRE),
            pltpu.VMEM((nd, deep, LANES), f32),
            pltpu.VMEM((everyone, deep, LANES), f32),
            pltpu.VMEM((nd, seqs, asked), f32),
            pltpu.VMEM((nd, seqs, asked), f32),
            dma((3 + 2 * seqs,)),
            dma((seqs,)), dma((seqs,)),
            dma((everyone,)), dma((everyone,)),
            dma((nd,)), dma((nd,)),
        ],
        compiler_params=pltpu.CompilerParams(
            collective_id=0, has_side_effects=True, vmem_limit_bytes=56_500_000
        ),
        name="scores",
    )(
        activations,
        out_grads,
        jnp.swapaxes(proj_in[0], 0, 1),
        jnp.swapaxes(proj_out[0], 0, 1),
        queries,
    )


def solution(mesh):
    placed = (
        P(None, ("parts", "dp"), None, ("tensor", "group")),
        P(None, ("parts", "dp"), None, ("tensor", "group")),
        P(None, ("tensor", "group"), None),
        P(None, ("tensor", "group"), None),
        P(("parts", "tensor", "group"), "dp"),
    )
    sizes = mesh.shape["dp"], mesh.shape["tensor"], mesh.shape["group"]

    def body(activations, out_grads, proj_in, proj_out, queries):
        layers, seqs = activations.shape[:2]
        rank = proj_in.shape[2]
        fits = (
            layers == 1
            and seqs == sizes[1] * sizes[2]
            and 2 * rank == LANES
            and rank % (2 * sizes[0]) == 0
        )
        run = functools.partial(fused, sizes) if fits else shards
        return run(activations, out_grads, proj_in, proj_out, queries)

    return jax.shard_map(
        body,
        mesh=mesh,
        in_specs=placed,
        out_specs=P("dp", ("parts", "tensor", "group")),
        check_vma=False,
    )
```

```python
import functools
import itertools

import jax
import jax.numpy as jnp
from jax import lax
from jax.experimental import pallas as pl
from jax.experimental.pallas import tpu as pltpu
from jax.sharding import PartitionSpec as P

MESH = pl.DeviceIdType.MESH
WIRE = jnp.bfloat16
NT = (((1,), (1,)), ((), ()))
LANES = 128


def shards(activations, out_grads, proj_in, proj_out, queries):
    proj_acts = jnp.einsum(
        "lsth,lhr->lstr", activations, proj_in, preferred_element_type=jnp.float32
    )
    proj_grads = jnp.einsum(
        "lsth,lhr->lstr", out_grads, proj_out, preferred_element_type=jnp.float32
    )
    summed_acts, summed_grads = lax.psum((proj_acts, proj_grads), ("tensor", "group"))
    outer = jnp.einsum(
        "lsta,lstb->slab",
        summed_grads.astype(jnp.bfloat16),
        summed_acts.astype(jnp.bfloat16),
        preferred_element_type=jnp.float32,
    )
    seq_count = outer.shape[0]
    example_grads = outer.reshape(seq_count, -1).astype(jnp.bfloat16)
    traded = lax.all_to_all(example_grads, "dp", split_axis=1, concat_axis=0, tiled=True)
    return lax.psum_scatter(
        lax.dot_general(
            traded, queries, (((1,), (1,)), ((), ())), preferred_element_type=jnp.float32
        ),
        "dp",
        scatter_dimension=0,
        tiled=True,
    )


def dot(left, right):
    return lax.dot_general(left, right, NT, preferred_element_type=jnp.float32)


def kernel(
    sizes,
    acts_hbm, grads_hbm, in_hbm, out_hbm, queries_hbm, scores_ref,
    acts, grads, w_in, w_out, queries, paired, own, sent, got, mine, feats, part, back,
    load_sem, send1, recv1, send2, recv2, send3, recv3,
):
    nd, nt, ng = sizes
    seqs, rank = nt * ng, w_in.shape[0]
    half = rank // 2
    d, t, g = lax.axis_index("dp"), lax.axis_index("tensor"), lax.axis_index("group")

    def peer(rd, rt, rg):
        return lax.rem(d + rd, nd), lax.rem(t + rt, nt), lax.rem(g + rg, ng)

    def device(where):
        return {"dp": where[0], "tensor": where[1], "group": where[2]}

    turns = sorted(itertools.product(range(nt), range(ng)), reverse=True)
    others = [r for r in itertools.product(range(nd), range(nt), range(ng)) if any(r)]
    others.sort(key=lambda r: (-r[0], -r[1], -r[2]))

    loads = [
        pltpu.make_async_copy(in_hbm, w_in, load_sem.at[0]),
        pltpu.make_async_copy(out_hbm, w_out, load_sem.at[1]),
    ]
    seq_loads = []
    for slot, (rt, rg) in enumerate(turns):
        _, pt, pg = peer(0, rt, rg)
        seq = pt * ng + pg
        seq_loads.append((
            pltpu.make_async_copy(acts_hbm.at[0, seq], acts.at[slot], load_sem.at[3 + 2 * slot]),
            pltpu.make_async_copy(grads_hbm.at[0, seq], grads.at[slot], load_sem.at[4 + 2 * slot]),
        ))
    query_load = pltpu.make_async_copy(queries_hbm, queries, load_sem.at[2])
    barrier = pltpu.get_barrier_semaphore()
    for r in others:
        pl.semaphore_signal(barrier, inc=1, device_id=device(peer(*r)), device_id_type=MESH)

    for copy in loads:
        copy.start()
    for pair in seq_loads:
        for copy in pair:
            copy.start()
    query_load.start()

    row = lax.broadcasted_iota(jnp.int32, (rank, rank), 0)
    column = lax.broadcasted_iota(jnp.int32, (rank, rank), 1)
    source = jnp.where(row < half, 2 * row, 2 * (row - half) + 1)
    pick = (column == source).astype(jnp.bfloat16)
    loads[1].wait()
    paired[...] = jnp.dot(
        pick, w_out[...], preferred_element_type=jnp.float32
    ).astype(jnp.bfloat16)
    loads[0].wait()

    first = []
    for slot, (rt, rg) in enumerate(turns):
        seq_loads[slot][0].wait()
        seq_loads[slot][1].wait()
        part_acts = dot(w_in[...], acts[slot])
        part_grads = dot(paired[...], grads[slot])
        if (rt, rg) == (0, 0):
            own[:rank] = part_acts
            own[rank:] = part_grads
            continue
        sent[slot, :rank] = part_acts.astype(sent.dtype)
        sent[slot, rank:] = part_grads.astype(sent.dtype)
        if not first:
            pl.semaphore_wait(barrier, len(others))
        copy = pltpu.make_async_remote_copy(
            src_ref=sent.at[slot],
            dst_ref=got.at[slot],
            send_sem=send1.at[slot],
            recv_sem=recv1.at[slot],
            device_id=device(peer(0, rt, rg)),
            device_id_type=MESH,
        )
        copy.start()
        first.append(copy)

    total = own[...]
    for slot, copy in enumerate(first):
        copy.wait_recv()
        total = total + got[slot].astype(jnp.float32)
    summed = total.astype(jnp.bfloat16)
    twice = jnp.concatenate([summed[:rank], summed[:rank]], axis=0)
    outer = dot(summed[rank:], twice)
    lane = lax.broadcasted_iota(jnp.int32, (half, 2 * rank), 1)
    eg = jnp.where(lane < rank, outer[:half], outer[half:])
    eg = eg.astype(jnp.bfloat16).astype(jnp.float32)
    deep = half // nd
    for other in range(nd):
        mine[other] = eg[other * deep:(other + 1) * deep]

    me = (d * nt + t) * ng + g
    second = []
    for at, r in enumerate(others):
        where = peer(*r)
        copy = pltpu.make_async_remote_copy(
            src_ref=mine.at[where[0]],
            dst_ref=feats.at[me],
            send_sem=send2.at[at],
            recv_sem=recv2.at[at],
            device_id=device(where),
            device_id_type=MESH,
        )
        copy.start()
        second.append(copy)
    feats[me] = mine[d]
    query_load.wait()
    for copy in second:
        copy.wait_recv()
    flat = jnp.concatenate([feats[:, k, :] for k in range(deep)], axis=1).astype(jnp.bfloat16)
    scores = dot(flat, queries[...])
    for other in range(nd):
        part[other] = scores[other * seqs:(other + 1) * seqs]

    third = []
    for rd in sorted(range(1, nd), key=lambda r: -min(r, nd - r)):
        where = peer(rd, 0, 0)
        copy = pltpu.make_async_remote_copy(
            src_ref=part.at[where[0]],
            dst_ref=back.at[rd - 1],
            send_sem=send3.at[rd - 1],
            recv_sem=recv3.at[rd - 1],
            device_id=device(where),
            device_id_type=MESH,
        )
        copy.start()
        third.append((rd, copy))
    result = part[d]
    for rd, copy in reversed(third):
        copy.wait_recv()
        result = result + back[rd - 1]
    scores_ref[...] = result
    for copy in first + second + [copy for _, copy in third]:
        copy.wait_send()


def fused(sizes, activations, out_grads, proj_in, proj_out, queries):
    nd, nt, ng = sizes
    seqs, tokens, width = activations.shape[1:]
    hidden, rank = out_grads.shape[3], proj_in.shape[2]
    asked, local = queries.shape
    everyone = nd * seqs
    deep = rank // 2 // nd
    bf16, f32 = jnp.bfloat16, jnp.float32
    dma = pltpu.SemaphoreType.DMA
    hbm = pl.BlockSpec(memory_space=pl.ANY)
    return pl.pallas_call(
        functools.partial(kernel, sizes),
        out_shape=jax.ShapeDtypeStruct((seqs, asked), f32),
        in_specs=[hbm] * 5,
        out_specs=pl.BlockSpec(memory_space=pltpu.VMEM),
        scratch_shapes=[
            pltpu.VMEM((seqs, tokens, width), bf16),
            pltpu.VMEM((seqs, tokens, hidden), bf16),
            pltpu.VMEM((rank, width), bf16),
            pltpu.VMEM((rank, hidden), bf16),
            pltpu.VMEM((asked, local), bf16),
            pltpu.VMEM((rank, hidden), bf16),
            pltpu.VMEM((2 * rank, tokens), f32),
            pltpu.VMEM((seqs, 2 * rank, tokens), WIRE),
            pltpu.VMEM((seqs, 2 * rank, tokens), WIRE),
            pltpu.VMEM((nd, deep, LANES), f32),
            pltpu.VMEM((everyone, deep, LANES), f32),
            pltpu.VMEM((nd, seqs, asked), f32),
            pltpu.VMEM((nd, seqs, asked), f32),
            dma((3 + 2 * seqs,)),
            dma((seqs,)), dma((seqs,)),
            dma((everyone,)), dma((everyone,)),
            dma((nd,)), dma((nd,)),
        ],
        compiler_params=pltpu.CompilerParams(
            collective_id=0, has_side_effects=True, vmem_limit_bytes=56_500_000
        ),
        name="scores",
    )(
        activations,
        out_grads,
        jnp.swapaxes(proj_in[0], 0, 1),
        jnp.swapaxes(proj_out[0], 0, 1),
        queries,
    )


def solution(mesh):
    placed = (
        P(None, ("parts", "dp"), None, ("tensor", "group")),
        P(None, ("parts", "dp"), None, ("tensor", "group")),
        P(None, ("tensor", "group"), None),
        P(None, ("tensor", "group"), None),
        P(("parts", "tensor", "group"), "dp"),
    )
    sizes = mesh.shape["dp"], mesh.shape["tensor"], mesh.shape["group"]

    def body(activations, out_grads, proj_in, proj_out, queries):
        layers, seqs = activations.shape[:2]
        rank = proj_in.shape[2]
        fits = (
            layers == 1
            and seqs == sizes[1] * sizes[2]
            and 2 * rank == LANES
            and rank % (2 * sizes[0]) == 0
        )
        run = functools.partial(fused, sizes) if fits else shards
        return run(activations, out_grads, proj_in, proj_out, queries)

    return jax.shard_map(
        body,
        mesh=mesh,
        in_specs=placed,
        out_specs=P("dp", ("parts", "tensor", "group")),
        check_vma=False,
    )
```
